32 devices in a mesh: fsdp: 4 (over y, core), ctx: 2 (over x), tp: 4 (over z).
Axes of the slice: x: 2, y: 2, z: 4, core: 2. Of those that a mesh axis runs over, the one named last changes fastest.
Arguments:
- inputs: bfloat16 [4096, 2048], P(('fsdp', 'ctx')), may hold values from -24 to 24
- seq_lengths: int32 [4, 4], P('fsdp'), may hold values from 1 to 768, 1024 in all within a row
- ln_gains: float32 [2, 2, 2048], replicated, may hold values from 0.5 to 1.5
- ln_biases: float32 [2, 2, 2048], replicated, may hold values from -4 to 4
- qkv_w: bfloat16 [2, 2048, 6144], P(None, 'fsdp', 'tp'), may hold values from -2 to 2
- qkv_b: float32 [2, 6144], P(None, 'tp'), may hold values from -6 to 6
- dense_w: bfloat16 [2, 2048, 2048], P(None, 'fsdp', 'tp'), may hold values from -1.5 to 1.5
- out_b: float32 [2, 2, 2048], replicated, may hold values from -4 to 4
- fc1_w: bfloat16 [2, 2048, 8192], P(None, 'fsdp', 'tp'), may hold values from -0.125 to 0.125
- fc1_b: float32 [2, 8192], P(None, 'tp'), may hold values from -6 to 6
- fc2_w: bfloat16 [2, 2048, 8192], P(None, 'fsdp', 'tp'), may hold values from -0.0625 to 0.0625
- out_grad: bfloat16 [4096, 2048], P(('fsdp', 'ctx')), may hold values from -6 to 6
Outputs:
- outputs: bfloat16 [4096, 2048], P(('fsdp', 'ctx'))
- input_grad: bfloat16 [4096, 2048], P(('fsdp', 'ctx'))
- ln_gain_grad: float32 [2, 2, 2048], replicated
- ln_bias_grad: float32 [2, 2, 2048], replicated
- qkv_w_grad: float32 [2, 2048, 6144], P(None, 'fsdp', 'tp')
- qkv_b_grad: float32 [2, 6144], P(None, 'tp')
- dense_w_grad: float32 [2, 2048, 2048], P(None, 'fsdp', 'tp')
- out_b_grad: float32 [2, 2, 2048], replicated
- fc1_w_grad: float32 [2, 2048, 8192], P(None, 'fsdp', 'tp')
- fc1_b_grad: float32 [2, 8192], P(None, 'tp')
- fc2_w_grad: float32 [2, 2048, 8192], P(None, 'fsdp', 'tp')
The draws below stay inside these ranges and needn't reach their ends.
Inputs may be any that keep to these rules, and one draw needn't show every extreme that they name: `seq_lengths`: each row gives, in order, the lengths of the 4 documents packed into the 1024 tokens of one sequence; they sum to 1024.
All inputs are finite; a program needn't handle non-finite values.
Results may differ from the reference program's by a relative error of at most 0.014.
Values may be sent and summed in bfloat16 or wider, within the bound.
No kernel may reach another device: no remote copies, remote signals or barrier semaphores. Data moves between devices by JAX's collectives and lax.ppermute only.
A program may use at most 448 MiB of HBM per device.

```python
import math
import jax
import jax.numpy as jnp
import numpy as np
from jax import lax

D = 2048
HEADS = 8
HD = 256
ROT = 64
FF = 8192
LAYERS = 2
SEQS = 4
GROUP = 1024
GROUPS = 4
TOKENS = 4096
MAXLEN = 768


def draw_inputs(key, part):
    base_key, row_key, col_key = jax.random.split(key, 3)
    row_scale = jnp.exp(jax.random.uniform(row_key, (TOKENS, 1), jnp.float32, math.log(0.3), math.log(3.0)))
    col_scale = jnp.exp(jax.random.uniform(col_key, (1, D), jnp.float32, math.log(0.5), math.log(2.0)))
    base_draw = jnp.clip(jax.random.normal(base_key, (TOKENS, D), jnp.float32), -4.0, 4.0)
    return (base_draw * row_scale * col_scale).astype(jnp.bfloat16)


def draw_qkv_w(key, part):
    noise = jnp.clip(jax.random.normal(key, (LAYERS, D, HEADS, 3, HD), jnp.float32), -3.0, 3.0) * D ** (-0.5)
    shaped = noise
    return shaped.reshape(LAYERS, D, 3 * D).astype(jnp.bfloat16)


def level_of(rng, extent, cuts, smallest, largest):
    def one(axis_at, parts):
        steps = jax.random.uniform(jax.random.fold_in(jax.random.fold_in(rng, 6), axis_at), (parts,), jnp.float32, smallest / len(cuts), largest / len(cuts))
        return jnp.repeat(jnp.exp(steps), extent[axis_at] // parts).reshape((-1,) + (1,) * (len(extent) - axis_at - 1))

    factor_of = one(*cuts[0])
    for cut in cuts[1:]:
        factor_of = factor_of * one(*cut)
    return factor_of


def profile(count, total, reach, slope):
    weights = [(1 << 20) // math.isqrt(standing ** slope) + 1 for standing in range(2, count + 1)]
    spare, given = total - reach - (count - 1), [1] * (count - 1)
    while spare > 0:
        free = [i for i in range(count - 1) if given[i] < reach]
        whole, remaining = sum([weights[i] for i in free]), spare
        for i in free:
            more = min(reach - given[i], max(1, remaining * weights[i] // whole), spare)
            given[i] = given[i] + more
            spare = spare - more
    return np.array([reach] + given)


def uneven_parts(rng, number_of, total, limit, skew):
    if number_of == 2:
        one = jax.random.randint(rng, (), max(1, total - limit), min(limit, total - 1) + 1)
        return jnp.stack([one, total - one])
    sizes = jnp.asarray(profile(number_of, total, limit, skew), jnp.int32)
    couples = (number_of - 1) // 2
    giver, receiver = sizes[1:1 + 2 * couples:2], sizes[2:2 + 2 * couples:2]
    slack = jnp.minimum(giver - 1, limit - receiver)
    passed = jax.random.randint(jax.random.fold_in(rng, 1), (couples,), 0, 1 << 20) % (slack + 1)
    sizes = sizes.at[1:1 + 2 * couples:2].set(giver - passed).at[2:2 + 2 * couples:2].set(receiver + passed)
    return sizes[jax.random.permutation(jax.random.fold_in(rng, 2), number_of)]


def bell_draw(own_key, shape, width, most, cuts=(), kind=jnp.bfloat16):
    entries = width * jax.random.normal(own_key, shape, jnp.float32)
    if cuts:
        entries = entries * level_of(own_key, shape, cuts, -0.22, 0.18)
    return jnp.clip(entries, -most, most).astype(kind)


def setup_inputs(seed: int = 0) -> dict:
    arg_keys = jax.random.split(jax.random.key(seed), 13)
    inputs = draw_inputs(jax.random.fold_in(arg_keys[12], 71), 0)
    seq_lengths = jax.vmap(lambda own: uneven_parts(own, SEQS, GROUP, MAXLEN, 2))(jax.random.split(arg_keys[1], GROUPS)).reshape((GROUPS, SEQS)).astype(jnp.int32)
    ln_gains = jnp.clip(1.0 + 0.1 * jax.random.normal(arg_keys[2], (LAYERS, 2, D), jnp.float32), 0.5, 1.5)
    ln_biases = bell_draw(arg_keys[3], (LAYERS, 2, D), 0.3, 4.0, (), jnp.float32)
    qkv_w = draw_qkv_w(jax.random.fold_in(arg_keys[12], 71), 0)
    qkv_b = bell_draw(arg_keys[5], (LAYERS, 3 * D), 0.5, 6.0, ((1, 4),), jnp.float32)
    dense_w = bell_draw(arg_keys[6], (LAYERS, D, D), (max(D // 128, 4)) ** -0.5, 1.5, ((1, 4), (2, 4)))
    out_b = bell_draw(arg_keys[7], (LAYERS, 2, D), 0.3, 4.0, (), jnp.float32)
    fc1_w = bell_draw(arg_keys[8], (LAYERS, D, FF), D ** -0.5, 0.125, ((1, 4), (2, 4)))
    fc1_b = bell_draw(arg_keys[9], (LAYERS, FF), 0.5, 6.0, ((1, 4),), jnp.float32)
    fc2_w = bell_draw(arg_keys[10], (LAYERS, D, FF), FF ** -0.5, 0.0625, ((1, 4), (2, 4)))
    out_grad = bell_draw(arg_keys[11], (TOKENS, D), 1.0, 6.0, ((0, 8),))
    return {"inputs": inputs, "seq_lengths": seq_lengths, "ln_gains": ln_gains, "ln_biases": ln_biases, "qkv_w": qkv_w, "qkv_b": qkv_b, "dense_w": dense_w, "out_b": out_b, "fc1_w": fc1_w, "fc1_b": fc1_b, "fc2_w": fc2_w, "out_grad": out_grad}


EPS = 1e-05
ROOT_HALF = 0.7071067811865476
INV_ROOT_TAU = 0.3989422804014327

def normal_cdf(values):
    return 0.5 * (1.0 + jax.scipy.special.erf(values * ROOT_HALF))

def gelu_slope(values):
    return normal_cdf(values) + values * jnp.exp(-0.5 * values * values) * INV_ROOT_TAU

def layer_norm(hidden, gain_row, shift_row):
    row_mean = lax.optimization_barrier(jnp.mean(hidden, axis=-1, keepdims=True))
    centred = hidden - row_mean
    row_var = lax.optimization_barrier(jnp.mean(centred * centred, axis=-1, keepdims=True))
    inv_std = lax.rsqrt(row_var + EPS)
    normed = centred * inv_std
    return ((normed * gain_row + shift_row).astype(jnp.bfloat16), normed, inv_std)

def norm_back(grads, normed, inv_std, gain_row):
    scaled = grads * gain_row
    return inv_std * (scaled - lax.optimization_barrier(jnp.mean(scaled, axis=-1, keepdims=True)) - normed * lax.optimization_barrier(jnp.mean(scaled * normed, axis=-1, keepdims=True)))

def rope_tables(positions):
    half_rot = ROT // 2
    inverse = 10000.0 ** (-(2.0 * jnp.arange(half_rot, dtype=jnp.float32)) / ROT)
    angles = positions.astype(jnp.float32)[:, None] * inverse[None, :]
    return (jnp.cos(angles)[:, None, :], jnp.sin(angles)[:, None, :])

def rotate(values, cosine, sine):
    half_rot = ROT // 2
    lower_half = values[..., :half_rot]
    upper_half = values[..., half_rot:ROT]
    return jnp.concatenate([lower_half * cosine - upper_half * sine, upper_half * cosine + lower_half * sine, values[..., ROT:]], axis=-1)

def rotate_back(grads, cosine, sine):
    half_rot = ROT // 2
    lower_half = grads[..., :half_rot]
    upper_half = grads[..., half_rot:ROT]
    return jnp.concatenate([lower_half * cosine + upper_half * sine, upper_half * cosine - lower_half * sine, grads[..., ROT:]], axis=-1)

def seq_tables(lengths, token_index, key_count):
    seq_ends = jnp.cumsum(lengths).astype(jnp.int32)
    starts = (seq_ends - lengths).astype(jnp.int32)
    segment = lax.optimization_barrier(jnp.sum((token_index[:, None] >= seq_ends[None, :]).astype(jnp.int32), axis=1)).astype(jnp.int32)
    seq_index = jnp.arange(lengths.shape[0], dtype=jnp.int32)
    seq_first = lax.optimization_barrier(jnp.sum(jnp.where(segment[:, None] == seq_index[None, :], starts[None, :], 0), axis=1)).astype(jnp.int32)
    key_index = jnp.arange(key_count, dtype=jnp.int32)
    allowed = (key_index[None, :] <= token_index[:, None]) & (key_index[None, :] >= seq_first[:, None])
    return ((token_index - seq_first).astype(jnp.int32), allowed)

def masked_scores(queries, key_rows, allowed, scale_factor):
    raw_scores = jnp.einsum('qhd,khd->hqk', queries.astype(jnp.float32), key_rows.astype(jnp.float32)) * scale_factor
    return jnp.where(allowed[None, :, :], raw_scores, -jnp.inf)

def reference(inputs, seq_lengths, ln_gains, ln_biases, qkv_w, qkv_b, dense_w, out_b, fc1_w, fc1_b, fc2_w, out_grad):
    scale_factor = HD ** (-0.5)

    def group_pass(carry, items):
        x_rows, lengths, cot_rows = items
        token_index = jnp.arange(GROUP, dtype=jnp.int32)
        positions, allowed = seq_tables(lengths, token_index, GROUP)
        cosine, sine = rope_tables(positions)
        hidden = x_rows.astype(jnp.float32)
        stored = []
        for layer_idx in range(LAYERS):
            attn_in, normed_a, inv_a = layer_norm(hidden, ln_gains[layer_idx, 0], ln_biases[layer_idx, 0])
            mlp_in, normed_m, inv_m = layer_norm(hidden, ln_gains[layer_idx, 1], ln_biases[layer_idx, 1])
            qkv_rows = (jnp.dot(attn_in, qkv_w[layer_idx], preferred_element_type=jnp.float32) + qkv_b[layer_idx]).reshape(GROUP, HEADS, 3, HD)
            queries = rotate(qkv_rows[:, :, 0], cosine, sine).astype(jnp.bfloat16)
            key_rows = rotate(qkv_rows[:, :, 1], cosine, sine).astype(jnp.bfloat16)
            value_rows = qkv_rows[:, :, 2].astype(jnp.bfloat16)
            scores = masked_scores(queries, key_rows, allowed, scale_factor)
            top_score = lax.optimization_barrier(jnp.max(scores, axis=-1, keepdims=True))
            log_total = top_score + jnp.log(lax.optimization_barrier(jnp.sum(jnp.exp(scores - top_score), axis=-1, keepdims=True)))
            prob_bf = jnp.exp(scores - log_total).astype(jnp.bfloat16)
            context = jnp.einsum('hqk,khd->qhd', prob_bf.astype(jnp.float32), value_rows.astype(jnp.float32)).astype(jnp.bfloat16).reshape(GROUP, D)
            attn_part = jnp.dot(context, dense_w[layer_idx].T, preferred_element_type=jnp.float32)
            pre_act = jnp.dot(mlp_in, fc1_w[layer_idx], preferred_element_type=jnp.float32) + fc1_b[layer_idx]
            activated = (pre_act * normal_cdf(pre_act)).astype(jnp.bfloat16)
            mlp_part = jnp.dot(activated, fc2_w[layer_idx].T, preferred_element_type=jnp.float32)
            stored.append((attn_in, normed_a, inv_a, mlp_in, normed_m, inv_m, queries, key_rows, value_rows, log_total, context, pre_act, activated))
            hidden = hidden + (attn_part + mlp_part) + out_b[layer_idx, 0] + out_b[layer_idx, 1]
        final_rows = hidden.astype(jnp.bfloat16)
        grad_rows = cot_rows.astype(jnp.float32)
        layer_grads = [None] * LAYERS
        for layer_idx in reversed(range(LAYERS)):
            attn_in, normed_a, inv_a, mlp_in, normed_m, inv_m, queries, key_rows, value_rows, log_total, context, pre_act, activated = stored[layer_idx]
            grad_bf = grad_rows.astype(jnp.bfloat16)
            grad_act = jnp.dot(grad_bf, fc2_w[layer_idx], preferred_element_type=jnp.float32)
            grad_pre = grad_act * gelu_slope(pre_act)
            grad_pre_bf = grad_pre.astype(jnp.bfloat16)
            mlp_back = jnp.dot(grad_pre_bf, fc1_w[layer_idx].T, preferred_element_type=jnp.float32)
            grad_ctx = jnp.dot(grad_bf, dense_w[layer_idx], preferred_element_type=jnp.float32).astype(jnp.bfloat16).reshape(GROUP, HEADS, HD)
            scores = masked_scores(queries, key_rows, allowed, scale_factor)
            probs = jnp.exp(scores - log_total)
            grad_prob = jnp.einsum('qhd,khd->hqk', grad_ctx.astype(jnp.float32), value_rows.astype(jnp.float32))
            row_delta = lax.optimization_barrier(jnp.sum(probs * grad_prob, axis=-1, keepdims=True))
            grad_score = (probs * (grad_prob - row_delta) * scale_factor).astype(jnp.bfloat16).astype(jnp.float32)
            grad_query = jnp.einsum('hqk,khd->qhd', grad_score, key_rows.astype(jnp.float32))
            grad_keys = jnp.einsum('hqk,qhd->khd', grad_score, queries.astype(jnp.float32))
            grad_values = jnp.einsum('hqk,qhd->khd', probs.astype(jnp.bfloat16).astype(jnp.float32), grad_ctx.astype(jnp.float32))
            grad_qkv = jnp.stack([rotate_back(grad_query, cosine, sine), rotate_back(grad_keys, cosine, sine), grad_values], axis=2).reshape(GROUP, 3 * D)
            grad_qkv_bf = grad_qkv.astype(jnp.bfloat16)
            attn_back = jnp.dot(grad_qkv_bf, qkv_w[layer_idx].T, preferred_element_type=jnp.float32)
            qkv_w_term = jnp.dot(attn_in.T, grad_qkv_bf, preferred_element_type=jnp.float32)
            dense_term = jnp.dot(grad_bf.T, context, preferred_element_type=jnp.float32)
            fc1_term = jnp.dot(mlp_in.T, grad_pre_bf, preferred_element_type=jnp.float32)
            fc2_term = jnp.dot(grad_bf.T, activated, preferred_element_type=jnp.float32)
            gain_term = jnp.stack([lax.optimization_barrier(jnp.sum(attn_back * normed_a, axis=0)), lax.optimization_barrier(jnp.sum(mlp_back * normed_m, axis=0))])
            shift_term = jnp.stack([lax.optimization_barrier(jnp.sum(attn_back, axis=0)), lax.optimization_barrier(jnp.sum(mlp_back, axis=0))])
            out_sum = lax.optimization_barrier(jnp.sum(grad_rows, axis=0))
            outb_term = jnp.stack([out_sum, out_sum])
            layer_grads[layer_idx] = (gain_term, shift_term, qkv_w_term, lax.optimization_barrier(jnp.sum(grad_qkv, axis=0)), dense_term, outb_term, fc1_term, lax.optimization_barrier(jnp.sum(grad_pre, axis=0)), fc2_term)
            grad_rows = grad_rows + norm_back(attn_back, normed_a, inv_a, ln_gains[layer_idx, 0]) + norm_back(mlp_back, normed_m, inv_m, ln_gains[layer_idx, 1])
        updated = []
        for item_idx in range(9):
            stacked = jnp.stack([layer_grads[layer_idx][item_idx] for layer_idx in range(LAYERS)])
            updated.append(carry[item_idx] + stacked)
        return (tuple(updated), (final_rows, grad_rows.astype(jnp.bfloat16)))
    initial = (jnp.zeros((LAYERS, 2, D), jnp.float32), jnp.zeros((LAYERS, 2, D), jnp.float32), jnp.zeros((LAYERS, D, 3 * D), jnp.float32), jnp.zeros((LAYERS, 3 * D), jnp.float32), jnp.zeros((LAYERS, D, D), jnp.float32), jnp.zeros((LAYERS, 2, D), jnp.float32), jnp.zeros((LAYERS, D, FF), jnp.float32), jnp.zeros((LAYERS, FF), jnp.float32), jnp.zeros((LAYERS, D, FF), jnp.float32))
    items = (inputs.reshape(GROUPS, GROUP, D), seq_lengths, out_grad.reshape(GROUPS, GROUP, D))
    totals, (final_all, grad_all) = lax.scan(group_pass, initial, items)
    return (final_all.reshape(TOKENS, D), grad_all.reshape(TOKENS, D), totals[0], totals[1], totals[2], totals[3], totals[4], totals[5], totals[6], totals[7], totals[8])
```

```python
import jax
import jax.numpy as jnp
from jax import lax
from jax.experimental import pallas as pl
from jax.experimental.pallas import tpu as pltpu
from jax.sharding import PartitionSpec as P

HD = 256
ROT = 64
LAYERS = 2
EPS = 1e-05
ROOT_HALF = 0.7071067811865476
INV_ROOT_TAU = 0.3989422804014327
BF = jnp.bfloat16
F32 = jnp.float32
TILE = 512
VMEM_BYTES = 58 * 2**20


NT = (((1,), (1,)), ((), ()))


def sds(shape, dtype):
    return jax.ShapeDtypeStruct(shape, dtype)


def full_spec(shape):
    return pl.BlockSpec(shape, lambda *_: (0,) * len(shape))


def params():
    return pltpu.CompilerParams(vmem_limit_bytes=VMEM_BYTES)


def cost(flops, arrays, transcendentals=0):
    total = 0
    for a in arrays:
        size = 1
        for n in a.shape:
            size *= n
        total += size * jnp.dtype(a.dtype).itemsize
    return pl.CostEstimate(flops=int(flops), bytes_accessed=int(total), transcendentals=int(transcendentals))


def normed_rows(hidden):
    row_mean = jnp.mean(hidden, axis=-1, keepdims=True)
    centred = hidden - row_mean
    row_var = jnp.mean(centred * centred, axis=-1, keepdims=True)
    inv_std = lax.rsqrt(row_var + EPS)
    return centred * inv_std, inv_std


def turn(values, cosine, sine, sign):
    front = values[:, :128]
    lane = lax.broadcasted_iota(jnp.int32, front.shape, 1)
    swapped = jnp.where(
        lane < ROT // 2,
        pltpu.roll(front, 128 - ROT // 2, 1),
        pltpu.roll(front, ROT // 2, 1),
    )
    front = front * cosine + (swapped * sine if sign > 0 else -(swapped * sine))
    return jnp.concatenate([front, values[:, 128:]], axis=1)


def piece_spec(piece, cols, at):
    array, layer, half, rows = piece
    if layer is not None:
        return pl.BlockSpec((None, rows, cols), lambda n, s: (layer, 0, at(n)))
    if half is not None:
        return pl.BlockSpec((rows, cols), lambda n, s: (s[0] ^ half, at(n)))
    return pl.BlockSpec((rows, cols), lambda n, s: (0, at(n)))


def piece_rows(ref, piece, s):
    _, layer, half, rows = piece
    if layer is not None:
        return ref.at[layer]
    if half is not None:
        return ref.at[pl.ds(pl.multiple_of((s[0] ^ half) * rows, rows), rows), :]
    return ref


def stacked(refs):
    parts = [r[...] for r in refs]
    return parts[0] if len(parts) == 1 else jnp.concatenate(parts, axis=0)


def first_norm(order, rows, inputs, out_grad, tp_rows):
    local, width = inputs.shape
    blocks, groups = order.shape[0], rows.shape[0]
    bw = width // blocks

    def kernel(order_ref, rows_ref, x_ref, g_ref, xhat_ref, own_ref, dy_ref):
        for k in range(groups):
            at = pl.ds(pl.multiple_of(rows_ref[k] * tp_rows, tp_rows), tp_rows)
            to = pl.ds(k * tp_rows, tp_rows)
            cols = [pl.ds(pl.multiple_of(order_ref[c] * bw, bw), bw) for c in range(blocks)]
            x = jnp.concatenate([x_ref[at, c] for c in cols], axis=1)
            if k == 0:
                own_ref[...] = x
            xhat_ref[to, :] = normed_rows(x.astype(F32))[0].astype(BF)
            for c in range(blocks):
                dy_ref[to, c * bw : (c + 1) * bw] = g_ref[at, cols[c]]

    smem = pl.BlockSpec(memory_space=pltpu.SMEM)
    vmem = pl.BlockSpec(memory_space=pltpu.VMEM)
    return pl.pallas_call(
        kernel,
        out_shape=(sds((local, width), BF), sds((tp_rows, width), BF), sds((local, width), BF)),
        in_specs=[smem, smem, vmem, vmem],
        out_specs=(vmem, vmem, vmem),
        compiler_params=params(),
        cost_estimate=cost(10 * local * width, [inputs] * 4),
        name="first_norm",
    )(order, rows, inputs, out_grad)


def qkv_forward(scal, xhats, vec, bias, cosine, sine, pieces):
    width = vec.shape[1]
    half = width // 2
    local = sum(x.shape[0] for x in xhats)
    heads = bias.shape[1] // (3 * HD)
    nx, nw = len(xhats), len(pieces)

    def kernel(s, *refs):
        xs, refs = refs[:nx], refs[nx:]
        vec_ref, bias_ref, cos_ref, sin_ref = refs[:4]
        ws, refs = refs[4 : 4 + nw], refs[4 + nw :]
        q_ref, kv_ref, a1e, a1o, a2e, a2o = refs

        @pl.when(pl.program_id(0) == 0)
        def _():
            at = 0
            for x in xs:
                n = x.shape[0]
                xhat = x[...].astype(F32)
                first = (xhat * vec_ref[0:1, :] + vec_ref[1:2, :]).astype(BF)
                second = (xhat * vec_ref[2:3, :] + vec_ref[3:4, :]).astype(BF)
                a1e[at : at + n, :] = first[:, :half]
                a1o[at : at + n, :] = first[:, half:]
                a2e[at : at + n, :] = second[:, :half]
                a2o[at : at + n, :] = second[:, half:]
                at += n

        lhs = jnp.concatenate([a1e[...], a1o[...]], axis=1)
        acc = jnp.dot(lhs, stacked(ws), preferred_element_type=F32) + bias_ref[...]
        cosv, sinv = cos_ref[...], sin_ref[...]
        q_ref[...] = turn(acc[:, :HD], cosv, sinv, 1).astype(BF)
        kv_ref[0] = turn(acc[:, HD : 2 * HD], cosv, sinv, 1).astype(BF)
        kv_ref[1] = acc[:, 2 * HD :].astype(BF)

    specs = [full_spec(x.shape) for x in xhats]
    specs += [full_spec(vec.shape), pl.BlockSpec((1, 3 * HD), lambda n, s: (0, n))]
    specs += [full_spec(cosine.shape), full_spec(sine.shape)]
    specs += [piece_spec(p, 3 * HD, lambda n: n) for p in pieces]
    arrays = [p[0] for p in pieces]
    outs = (
        sds((heads, local, HD), BF),
        sds((2, heads, local, HD), BF),
        *(sds((local, half), BF) for _ in range(4)),
    )
    return pl.pallas_call(
        kernel,
        out_shape=outs,
        grid_spec=pltpu.PrefetchScalarGridSpec(
            num_scalar_prefetch=1,
            grid=(heads,),
            in_specs=specs,
            out_specs=(
                pl.BlockSpec((None, local, HD), lambda n, s: (n, 0, 0)),
                pl.BlockSpec((2, None, local, HD), lambda n, s: (0, n, 0, 0)),
                *(full_spec((local, half)) for _ in range(4)),
            ),
        ),
        compiler_params=params(),
        cost_estimate=cost(2 * local * width * bias.shape[1], [*outs, *xhats, sds((width, bias.shape[1]), BF)]),
        name="qkv_forward",
    )(scal, *xhats, vec, bias, cosine, sine, *arrays)


def hidden_forward(scal, a_even, a_odd, bias, pieces):
    local, half = a_even.shape
    units = bias.shape[1]
    nw = len(pieces)

    def kernel(s, ae, ao, bias_ref, *refs):
        ws, (act_ref, slope_ref) = refs[:nw], refs[nw:]
        lhs = jnp.concatenate([ae[...], ao[...]], axis=1)
        fc = jnp.dot(lhs, stacked(ws), preferred_element_type=F32) + bias_ref[...]
        cdf = 0.5 * (1.0 + lax.erf(fc * ROOT_HALF))
        act_ref[...] = (fc * cdf).astype(BF)
        slope_ref[...] = (cdf + fc * jnp.exp(-0.5 * fc * fc) * INV_ROOT_TAU).astype(BF)

    specs = [full_spec(a_even.shape), full_spec(a_odd.shape), pl.BlockSpec((1, TILE), lambda n, s: (0, n))]
    specs += [piece_spec(p, TILE, lambda n: n) for p in pieces]
    outs = (sds((local, units), BF), sds((local, units), BF))
    return pl.pallas_call(
        kernel,
        out_shape=outs,
        grid_spec=pltpu.PrefetchScalarGridSpec(
            num_scalar_prefetch=1,
            grid=(units // TILE,),
            in_specs=specs,
            out_specs=tuple(pl.BlockSpec((local, TILE), lambda n, s: (0, n)) for _ in range(2)),
        ),
        compiler_params=params(),
        cost_estimate=cost(
            4 * local * half * units, [*outs, a_even, a_odd, sds((2 * half, units), BF)], 2 * local * units
        ),
        name="hidden_forward",
    )(scal, a_even, a_odd, bias, *[p[0] for p in pieces])


def allowed_of(query_ref, first_ref, key_ref):
    keys = key_ref[...]
    return (keys <= query_ref[...]) & (keys >= first_ref[...])


def attend(q, kv, kv_far, marks):
    heads, local, _ = q.shape
    scale = HD ** (-0.5)

    def kernel(tq, fq, kn, kf, q_ref, kv_ref, far_ref, ctx_ref, lse_ref):
        query = q_ref[...]
        near = lax.dot_general(query, kv_ref[0], NT, preferred_element_type=F32) * scale
        far = lax.dot_general(query, far_ref[0], NT, preferred_element_type=F32) * scale
        near = jnp.where(allowed_of(tq, fq, kn), near, -jnp.inf)
        far = jnp.where(allowed_of(tq, fq, kf), far, -jnp.inf)
        top = jnp.maximum(jnp.max(near, axis=1, keepdims=True), jnp.max(far, axis=1, keepdims=True))
        near, far = jnp.exp(near - top), jnp.exp(far - top)
        total = jnp.sum(near, axis=1, keepdims=True) + jnp.sum(far, axis=1, keepdims=True)
        inv = 1.0 / total
        lse_ref[...] = top + jnp.log(total)
        ctx = jnp.dot((near * inv).astype(BF), kv_ref[1], preferred_element_type=F32)
        ctx += jnp.dot((far * inv).astype(BF), far_ref[1], preferred_element_type=F32)
        ctx_ref[...] = ctx.astype(BF)

    kv_spec = pl.BlockSpec((2, None, local, HD), lambda n: (0, n, 0, 0))
    outs = (sds((local, heads * HD), BF), sds((heads, local, 1), F32))
    return pl.pallas_call(
        kernel,
        out_shape=outs,
        grid=(heads,),
        in_specs=[full_spec(m.shape) for m in marks]
        + [pl.BlockSpec((None, local, HD), lambda n: (n, 0, 0)), kv_spec, kv_spec],
        out_specs=(
            pl.BlockSpec((local, HD), lambda n: (0, n)),
            pl.BlockSpec((None, local, 1), lambda n: (n, 0, 0)),
        ),
        compiler_params=params(),
        cost_estimate=cost(8 * heads * local * local * HD, [*outs, q, kv, kv_far], 2 * heads * local * local),
        name="attend",
    )(*marks, q, kv, kv_far)


def attend_back(q, kv, kv_far, grad_ctx, lse, marks, cosine, sine):
    heads, local, _ = q.shape
    scale = HD ** (-0.5)
    tn = (((0,), (0,)), ((), ()))

    def kernel(tq, fq, kn, kf, cos_ref, sin_ref, q_ref, kv_ref, far_ref, g_ref, lse_ref, *outs):
        dq_ref, sum_ref, near_ref, away_ref = outs
        query, grad = q_ref[...], g_ref[...]
        probs, grads = [], []
        for ref, mark in ((kv_ref, kn), (far_ref, kf)):
            score = lax.dot_general(query, ref[0], NT, preferred_element_type=F32) * scale
            score = jnp.where(allowed_of(tq, fq, mark), score, -jnp.inf)
            probs.append(jnp.exp(score - lse_ref[...]))
            grads.append(lax.dot_general(grad, ref[1], NT, preferred_element_type=F32))
        delta = jnp.sum(probs[0] * grads[0], axis=1, keepdims=True)
        delta += jnp.sum(probs[1] * grads[1], axis=1, keepdims=True)
        dscore = [(p * (g - delta) * scale).astype(BF) for p, g in zip(probs, grads)]
        probb = [p.astype(BF) for p in probs]
        dq = jnp.dot(dscore[0], kv_ref[0], preferred_element_type=F32)
        dq += jnp.dot(dscore[1], far_ref[0], preferred_element_type=F32)
        dq = turn(dq, cos_ref[...], sin_ref[...], -1)
        dq_ref[...] = dq.astype(BF)
        sum_ref[...] = jnp.sum(dq, axis=0, keepdims=True)
        near_ref[0] = lax.dot_general(dscore[0], query, tn, preferred_element_type=F32)
        near_ref[1] = lax.dot_general(probb[0], grad, tn, preferred_element_type=F32)
        away_ref[0] = lax.dot_general(dscore[1], query, tn, preferred_element_type=F32).astype(BF)
        away_ref[1] = lax.dot_general(probb[1], grad, tn, preferred_element_type=F32).astype(BF)

    kv_spec = pl.BlockSpec((2, None, local, HD), lambda n: (0, n, 0, 0))
    outs = (
        sds((local, heads * HD), BF),
        sds((heads, 1, HD), F32),
        sds((2, heads, local, HD), F32),
        sds((2, heads, local, HD), BF),
    )
    return pl.pallas_call(
        kernel,
        out_shape=outs,
        grid=(heads,),
        in_specs=[full_spec(m.shape) for m in (*marks, cosine, sine)]
        + [
            pl.BlockSpec((None, local, HD), lambda n: (n, 0, 0)),
            kv_spec,
            kv_spec,
            pl.BlockSpec((local, HD), lambda n: (0, n)),
            pl.BlockSpec((None, local, 1), lambda n: (n, 0, 0)),
        ],
        out_specs=(
            pl.BlockSpec((local, HD), lambda n: (0, n)),
            pl.BlockSpec((None, 1, HD), lambda n: (n, 0, 0)),
            kv_spec,
            kv_spec,
        ),
        compiler_params=params(),
        cost_estimate=cost(20 * heads * local * local * HD, [*outs, q, kv, kv_far, grad_ctx], 2 * heads * local * local),
        name="attend_back",
    )(*marks, cosine, sine, q, kv, kv_far, grad_ctx, lse)


def join_qkv_grads(dq, dq_sum, near, arrived, cosine, sine):
    _, heads, local, _ = near.shape

    def kernel(cos_ref, sin_ref, dq_ref, s_ref, near_ref, far_ref, out_ref, sum_ref):
        dk = turn(near_ref[0] + far_ref[0].astype(F32), cos_ref[...], sin_ref[...], -1)
        dv = near_ref[1] + far_ref[1].astype(F32)
        out_ref[:, :HD] = dq_ref[...]
        out_ref[:, HD : 2 * HD] = dk.astype(BF)
        out_ref[:, 2 * HD :] = dv.astype(BF)
        sum_ref[:, :HD] = s_ref[...]
        sum_ref[:, HD : 2 * HD] = jnp.sum(dk, axis=0, keepdims=True)
        sum_ref[:, 2 * HD :] = jnp.sum(dv, axis=0, keepdims=True)

    kv_spec = pl.BlockSpec((2, None, local, HD), lambda n: (0, n, 0, 0))
    outs = (sds((local, 3 * heads * HD), BF), sds((1, 3 * heads * HD), F32))
    return pl.pallas_call(
        kernel,
        out_shape=outs,
        grid=(heads,),
        in_specs=[
            full_spec(cosine.shape),
            full_spec(sine.shape),
            pl.BlockSpec((local, HD), lambda n: (0, n)),
            pl.BlockSpec((None, 1, HD), lambda n: (n, 0, 0)),
            kv_spec,
            kv_spec,
        ],
        out_specs=(
            pl.BlockSpec((local, 3 * HD), lambda n: (0, n)),
            pl.BlockSpec((1, 3 * HD), lambda n: (0, n)),
        ),
        compiler_params=params(),
        cost_estimate=cost(10 * heads * local * HD, [*outs, dq, near, arrived]),
        name="join_qkv_grads",
    )(cosine, sine, dq, dq_sum, near, arrived)


def tiles_of(first, second):
    tiles, rows = [[]], 0
    for i, (a, b) in enumerate(zip(first, second)):
        if rows + a[3] > TILE:
            tiles.append([])
            rows = 0
        tiles[-1].append((i, rows, a, b))
        rows += a[3]
    return tiles


def streamed(s, tiles, refs_a, refs_b, buf_a, buf_b, sems, step):
    def copies(t):
        slot, out = t % 2, []
        for j, (i, row, a, b) in enumerate(tiles[t]):
            for m, (refs, piece, buf) in enumerate(((refs_a, a, buf_a), (refs_b, b, buf_b))):
                out.append(
                    pltpu.make_async_copy(
                        piece_rows(refs[i], piece, s), buf.at[slot, pl.ds(row, piece[3]), :], sems.at[slot, 2 * j + m]
                    )
                )
        return out

    flying = copies(0)
    for c in flying:
        c.start()
    for t in range(len(tiles)):
        later = []
        if t + 1 < len(tiles):
            later = copies(t + 1)
            for c in later:
                c.start()
        for c in flying:
            c.wait()
        flying = later
        step(t, t % 2)


def branch_out(scal, ctx, act, dense, fc2, groups):
    local, units = act.shape
    heads_cols = ctx.shape[1]
    width = sum(p[3] for p in fc2)
    tp_rows = local // groups
    tiles = tiles_of(dense, fc2)
    n = len(fc2)
    starts = [sum(p[3] for tile in tiles[:t] for (_, _, p, _) in tile) for t in range(len(tiles))]
    most = max(len(t) for t in tiles)

    def kernel(s, ctx_ref, act_ref, *refs):
        ds, fs = refs[:n], refs[n : 2 * n]
        outs, (buf_d, buf_f, sems) = refs[2 * n : 2 * n + groups], refs[2 * n + groups :]

        def step(t, slot):
            rows = sum(p[3] for (_, _, p, _) in tiles[t])
            acc = lax.dot_general(act_ref[...], buf_f[slot], NT, preferred_element_type=F32)
            acc += lax.dot_general(ctx_ref[...], buf_d[slot], NT, preferred_element_type=F32)
            for k in range(groups):
                part = acc[k * tp_rows : (k + 1) * tp_rows, :rows]
                outs[k][:, starts[t] : starts[t] + rows] = part.astype(outs[k].dtype)

        streamed(s, tiles, ds, fs, buf_d, buf_f, sems, step)

    outs = tuple(sds((tp_rows, width), F32 if k == 0 else BF) for k in range(groups))
    return pl.pallas_call(
        kernel,
        out_shape=outs,
        in_specs=[pl.BlockSpec(memory_space=pltpu.SMEM)]
        + [pl.BlockSpec(memory_space=pltpu.VMEM)] * 2
        + [pl.BlockSpec(memory_space=pl.ANY)] * (2 * n),
        out_specs=tuple(pl.BlockSpec(memory_space=pltpu.VMEM) for _ in outs),
        scratch_shapes=[
            pltpu.VMEM((2, TILE, heads_cols), BF),
            pltpu.VMEM((2, TILE, units), BF),
            pltpu.SemaphoreType.DMA((2, 2 * most)),
        ],
        compiler_params=params(),
        cost_estimate=cost(
            2 * local * width * (units + heads_cols), [*outs, ctx, act, sds((width, units + heads_cols), BF)]
        ),
        name="branch_out",
    )(scal, ctx, act, *[p[0] for p in dense], *[p[0] for p in fc2])


def row_kernel(kernel, outs, args, name):
    vmem = pl.BlockSpec(memory_space=pltpu.VMEM)
    return pl.pallas_call(
        kernel,
        out_shape=outs,
        in_specs=[vmem] * len(args),
        out_specs=tuple(vmem for _ in outs),
        compiler_params=params(),
        cost_estimate=cost(20 * args[0].shape[0] * args[0].shape[1], [*outs, *args]),
        name=name,
    )(*args)


def add_norm(hidden, own, arrived, biases, last):
    n = len(arrived)

    def kernel(h_ref, o_ref, b_ref, *refs):
        total = o_ref[...]
        for r in refs[:n]:
            total += r[...].astype(F32)
        new = h_ref[...].astype(F32) + total + b_ref[0:1, :] + b_ref[1:2, :]
        if last:
            refs[n][...] = new.astype(BF)
        else:
            refs[n][...] = new
            refs[n + 1][...] = normed_rows(new)[0].astype(BF)

    shape = own.shape
    outs = (sds(shape, BF),) if last else (sds(shape, F32), sds(shape, BF))
    return row_kernel(kernel, outs, [hidden, own, biases, *arrived], "add_norm")


def norm_back(grad, hidden, own, arrived, last):
    n = len(arrived)

    def kernel(g_ref, h_ref, o_ref, *refs):
        s = o_ref[...]
        for r in refs[:n]:
            s += r[...].astype(F32)
        xhat, inv_std = normed_rows(h_ref[...].astype(F32))
        grad_in = g_ref[...].astype(F32)
        mean_s = jnp.mean(s, axis=-1, keepdims=True)
        mean_sx = jnp.mean(s * xhat, axis=-1, keepdims=True)
        new = grad_in + inv_std * (s - mean_s - xhat * mean_sx)
        refs[n][...] = jnp.sum(grad_in, axis=0, keepdims=True)
        refs[n + 1][...] = new.astype(BF)
        if not last:
            refs[n + 2][...] = new

    rows, width = own.shape
    outs = (sds((1, width), F32), sds((rows, width), BF))
    if not last:
        outs += (sds((rows, width), F32),)
    return row_kernel(kernel, outs, [grad, hidden, own, *arrived], "norm_back")


def hidden_back(scal, dys, slope, fc2, dense):
    local, units = slope.shape
    width = sum(p[3] for p in fc2)
    half = width // 2
    ctx_cols = dense[0][0].shape[-1]
    steps = units // TILE
    nd, nw = len(dys), len(fc2)

    def kernel(s, *refs):
        ds, slope_ref, refs = refs[:nd], refs[nd], refs[nd + 1 :]
        fs, es, outs = refs[:nw], refs[nw : 2 * nw], refs[2 * nw :]
        grad_ref, sum_ref, ctx_ref, even, odd = outs
        i = pl.program_id(0)

        @pl.when(i == 0)
        def _():
            at = 0
            for d in ds:
                n = d.shape[0]
                even[at : at + n, :] = d[:, :half]
                odd[at : at + n, :] = d[:, half:]
                at += n

        @pl.when(i < steps)
        def _():
            lhs = jnp.concatenate([even[...], odd[...]], axis=1)
            acc = jnp.dot(lhs, stacked(fs), preferred_element_type=F32)
            acc = acc * slope_ref[...].astype(F32)
            grad_ref[...] = acc.astype(BF)
            sum_ref[...] = jnp.sum(acc, axis=0, keepdims=True)

        @pl.when(i >= steps)
        def _():
            lhs = jnp.concatenate([even[...], odd[...]], axis=1)
            ctx_ref[...] = jnp.dot(lhs, stacked(es), preferred_element_type=F32).astype(BF)

    near = lambda n: jnp.minimum(n, steps - 1)
    specs = [full_spec(d.shape) for d in dys]
    specs += [pl.BlockSpec((local, TILE), lambda n, s: (0, near(n)))]
    specs += [piece_spec(p, TILE, near) for p in fc2]
    specs += [piece_spec(p, ctx_cols, lambda n: 0) for p in dense]
    outs = (
        sds((local, units), BF),
        sds((1, units), F32),
        sds((local, ctx_cols), BF),
        sds((local, half), BF),
        sds((local, half), BF),
    )
    return pl.pallas_call(
        kernel,
        out_shape=outs,
        grid_spec=pltpu.PrefetchScalarGridSpec(
            num_scalar_prefetch=1,
            grid=(steps + 1,),
            in_specs=specs,
            out_specs=(
                pl.BlockSpec((local, TILE), lambda n, s: (0, near(n))),
                pl.BlockSpec((1, TILE), lambda n, s: (0, near(n))),
                full_spec((local, ctx_cols)),
                full_spec((local, half)),
                full_spec((local, half)),
            ),
        ),
        compiler_params=params(),
        cost_estimate=cost(
            2 * local * width * (units + ctx_cols), [*outs, *dys, slope, sds((width, units + ctx_cols), BF)]
        ),
        name="hidden_back",
    )(scal, *dys, slope, *[p[0] for p in fc2], *[p[0] for p in dense])


def normed_grads(scal, dqkv, dfc, xhats, vec, qkv, fc1, groups):
    local, units = dfc.shape
    qkv_cols = dqkv.shape[1]
    width = vec.shape[1]
    tp_rows = local // groups
    tiles = tiles_of(qkv, fc1)
    n, nx = len(qkv), len(xhats)
    starts = [sum(p[3] for tile in tiles[:t] for (_, _, p, _) in tile) for t in range(len(tiles))]
    most = max(len(t) for t in tiles)

    def kernel(s, dqkv_ref, dfc_ref, vec_ref, *refs):
        xs, refs = refs[:nx], refs[nx:]
        qs, fs = refs[:n], refs[n : 2 * n]
        outs, sum_ref = refs[2 * n : 2 * n + groups], refs[2 * n + groups]
        buf_q, buf_f, sems = refs[2 * n + groups + 1 :]

        def step(t, slot):
            rows = sum(p[3] for (_, _, p, _) in tiles[t])
            cols = slice(starts[t], starts[t] + rows)
            xhat = jnp.concatenate([x[:, cols] for x in xs], axis=0).astype(F32)
            first = lax.dot_general(dqkv_ref[...], buf_q[slot], NT, preferred_element_type=F32)[:, :rows]
            sum_ref[0:1, cols] = jnp.sum(first * xhat, axis=0, keepdims=True)
            sum_ref[2:3, cols] = jnp.sum(first, axis=0, keepdims=True)
            total = first * vec_ref[0:1, cols]
            second = lax.dot_general(dfc_ref[...], buf_f[slot], NT, preferred_element_type=F32)[:, :rows]
            sum_ref[1:2, cols] = jnp.sum(second * xhat, axis=0, keepdims=True)
            sum_ref[3:4, cols] = jnp.sum(second, axis=0, keepdims=True)
            total += second * vec_ref[2:3, cols]
            for k in range(groups):
                outs[k][:, cols] = total[k * tp_rows : (k + 1) * tp_rows, :].astype(outs[k].dtype)

        streamed(s, tiles, qs, fs, buf_q, buf_f, sems, step)

    outs = tuple(sds((tp_rows, width), F32 if k == 0 else BF) for k in range(groups)) + (sds((4, width), F32),)
    vmem = pl.BlockSpec(memory_space=pltpu.VMEM)
    return pl.pallas_call(
        kernel,
        out_shape=outs,
        in_specs=[pl.BlockSpec(memory_space=pltpu.SMEM)]
        + [vmem] * (3 + nx)
        + [pl.BlockSpec(memory_space=pl.ANY)] * (2 * n),
        out_specs=tuple(vmem for _ in outs),
        scratch_shapes=[
            pltpu.VMEM((2, TILE, qkv_cols), BF),
            pltpu.VMEM((2, TILE, units), BF),
            pltpu.SemaphoreType.DMA((2, 2 * most)),
        ],
        compiler_params=params(),
        cost_estimate=cost(
            2 * local * width * (units + qkv_cols), [*outs, dqkv, dfc, *xhats, sds((width, units + qkv_cols), BF)]
        ),
        name="normed_grads",
    )(scal, dqkv, dfc, vec, *xhats, *[p[0] for p in qkv], *[p[0] for p in fc1])


def weight_grad(scal, left, left_far, start, rows, right, right_far, arrived, swap_rows, name):
    tokens = left.shape[0]
    cols = right.shape[1]
    n = len(arrived)
    block = rows if start == 0 and n else swap_rows

    def kernel(s, l_ref, m_ref, r_ref, q_ref, *refs):
        out_ref, flipped = refs[n], refs[n + 1]

        @pl.when(pl.program_id(0) == 0)
        def _():
            for h in range(rows // block):
                if block == rows or swap_rows == rows:
                    to = pl.ds(h * block, block)
                else:
                    to = pl.ds(pl.multiple_of((h ^ s[0]) * block, block), block)
                cols_at = slice(start + h * block, start + (h + 1) * block)
                flipped[to, :tokens] = l_ref[:, cols_at].T
                flipped[to, tokens:] = m_ref[:, cols_at].T

        rhs = jnp.concatenate([r_ref[...], q_ref[...]], axis=0)
        acc = jnp.dot(flipped[...], rhs, preferred_element_type=F32)
        for r in refs[:n]:
            acc += r[...].astype(F32)
        out_ref[...] = acc.astype(BF)

    tile = min(TILE, cols)
    out = sds((rows, cols), BF)
    col_spec = lambda r: pl.BlockSpec((r, tile), lambda i, s: (0, i))
    return pl.pallas_call(
        kernel,
        out_shape=out,
        grid_spec=pltpu.PrefetchScalarGridSpec(
            num_scalar_prefetch=1,
            grid=(cols // tile,),
            in_specs=[full_spec(left.shape)] * 2 + [col_spec(tokens)] * 2 + [col_spec(rows)] * n,
            out_specs=col_spec(rows),
            scratch_shapes=[pltpu.VMEM((rows, 2 * tokens), BF)],
        ),
        compiler_params=params(),
        cost_estimate=cost(4 * tokens * rows * cols, [out, left, left_far, right, right_far, *arrived]),
        name=name,
    )(scal, left, left_far, right, right_far, *arrived)


def finish_grad(mine, arrived, layer, held):
    rows, cols = mine.shape
    tile = min(rows, 128)
    spec = pl.BlockSpec((tile, cols), lambda i: (i, 0))
    out_spec = pl.BlockSpec((None, tile, cols), lambda i: (layer, i, 0))

    def kernel(a_ref, b_ref, *refs):
        refs[-1][...] = a_ref[...].astype(F32) + b_ref[...].astype(F32)

    args = [mine, arrived] + ([] if held is None else [held])
    return pl.pallas_call(
        kernel,
        out_shape=sds((LAYERS, rows, cols), F32),
        grid=(rows // tile,),
        in_specs=[spec, spec] + ([] if held is None else [pl.BlockSpec(memory_space=pl.ANY)]),
        out_specs=out_spec,
        input_output_aliases={} if held is None else {2: 0},
        compiler_params=params(),
        cost_estimate=cost(rows * cols, [mine, arrived, mine, mine]),
        name="finish_grad",
    )(*args)


def place_rows(order, rows, parts):
    tp_rows, width = parts[0].shape
    blocks, groups = order.shape[0], len(parts)
    bw = width // blocks

    def kernel(order_ref, rows_ref, *refs):
        out_ref = refs[groups]
        for k in range(groups):
            at = pl.ds(pl.multiple_of(rows_ref[k] * tp_rows, tp_rows), tp_rows)
            for c in range(blocks):
                to = pl.ds(pl.multiple_of(order_ref[c] * bw, bw), bw)
                out_ref[at, to] = refs[k][:, c * bw : (c + 1) * bw]

    smem = pl.BlockSpec(memory_space=pltpu.SMEM)
    vmem = pl.BlockSpec(memory_space=pltpu.VMEM)
    return pl.pallas_call(
        kernel,
        out_shape=sds((tp_rows * groups, width), BF),
        in_specs=[smem, smem] + [vmem] * groups,
        out_specs=vmem,
        compiler_params=params(),
        cost_estimate=cost(0, [*parts, *parts]),
        name="place_rows",
    )(order, rows, *parts)


def per_device(
    inputs,
    seq_lengths,
    ln_gains,
    ln_biases,
    qkv_w,
    qkv_b,
    dense_w,
    out_b,
    fc1_w,
    fc1_b,
    fc2_w,
    out_grad,
):
    shards, sides, groups = lax.axis_size("fsdp"), lax.axis_size("ctx"), lax.axis_size("tp")
    assert sides == 2 and shards % 2 == 0
    f, x, z = lax.axis_index("fsdp"), lax.axis_index("ctx"), lax.axis_index("tp")
    local, width = inputs.shape
    block = width // shards
    tp_rows = local // groups
    share = (block // 2) % 128 == 0

    def swap(values, axis, bit):
        size = {"fsdp": shards, "ctx": sides, "tp": groups}[axis]
        return lax.ppermute(values, axis, [(i, i ^ bit) for i in range(size)])

    js = [*range(0, shards, 2), *range(1, shards, 2)]
    jarr = jnp.array(js, jnp.int32)
    if share:
        halves = jnp.arange(2, dtype=jnp.int32)
        order = ((f ^ jarr) * 2)[:, None] + (halves[None, :] ^ jnp.where(jarr >= 2, x, 0)[:, None])
        order = order.reshape(-1).astype(jnp.int32)
    else:
        order = (f ^ jarr).astype(jnp.int32)
    back_order = jnp.argsort(order).astype(jnp.int32)
    bw = width // order.shape[0]
    rows = (z ^ jnp.arange(groups, dtype=jnp.int32)).astype(jnp.int32)
    scal = jnp.reshape(x, (1,)).astype(jnp.int32)

    def reorder(vectors, index):
        lead = vectors.shape[0]
        return jnp.take(vectors.reshape(lead, -1, bw), index, axis=1).reshape(lead, width)

    matrices = {"qkv": qkv_w, "fc1": fc1_w, "fc2": fc2_w, "dense": dense_w}
    core = {m: swap(w, "fsdp", 1) for m, w in matrices.items()}
    pieces = {}
    for layer in range(LAYERS):
        for m, w in matrices.items():
            held = {0: [(w, layer, None, block)], 1: [(core[m], layer, None, block)]}
            for j in range(2, shards, 2):
                if share and layer == 0:
                    mine = lax.dynamic_slice_in_dim(w[layer], x * (block // 2), block // 2, 0)
                    near = swap(mine, "fsdp", j)
                    got = [near, swap(near, "ctx", 1)]
                    held[j] = [(g, None, None, block // 2) for g in got]
                    held[j + 1] = [(swap(g, "fsdp", 1), None, None, block // 2) for g in got]
                else:
                    near = swap(w[layer], "fsdp", j)
                    for k, g in ((j, near), (j + 1, swap(near, "fsdp", 1))):
                        if share:
                            held[k] = [(g, None, h, block // 2) for h in range(2)]
                        else:
                            held[k] = [(g, None, None, block)]
            pieces[m, layer] = [p for j in js for p in held[j]]

    spread = (rows[:, None] * tp_rows + jnp.arange(tp_rows, dtype=jnp.int32)[None, :]).reshape(-1)
    token = x * local + spread
    far_token = (1 - x) * local + spread
    ends = jnp.cumsum(seq_lengths[0])
    starts = ends - seq_lengths[0]
    segment = jnp.sum((token[:, None] >= ends[None, :]).astype(jnp.int32), axis=1)
    which = jnp.arange(ends.shape[0], dtype=jnp.int32)
    first = jnp.sum(jnp.where(segment[:, None] == which[None, :], starts[None, :], 0), axis=1)
    inverse = 10000.0 ** (-(2.0 * jnp.arange(ROT // 2, dtype=F32)) / ROT)
    angles = (token - first).astype(F32)[:, None] * inverse[None, :]
    cos, sin = jnp.cos(angles), jnp.sin(angles)
    rest = 128 - ROT
    cosine = jnp.concatenate([cos, cos, jnp.ones((local, rest), F32)], axis=1)
    sine = jnp.concatenate([-sin, sin, jnp.zeros((local, rest), F32)], axis=1)
    marks = (token[:, None], first[:, None], token[None, :], far_token[None, :])

    lnv = jnp.stack([ln_gains[:, 0], ln_biases[:, 0], ln_gains[:, 1], ln_biases[:, 1]], axis=1)
    vecs = reorder(jnp.concatenate([lnv.reshape(-1, width), out_b.reshape(-1, width)], axis=0), order)
    lnv = [vecs[4 * i : 4 * i + 4] for i in range(LAYERS)]
    outv = [vecs[4 * LAYERS + 2 * i : 4 * LAYERS + 2 * i + 2] for i in range(LAYERS)]

    xhat, own_rows, dy = first_norm(order, rows, inputs, out_grad, tp_rows)
    xhats, hidden = [xhat], own_rows
    saved = []
    for layer in range(LAYERS):
        q, kv, a1e, a1o, a2e, a2o = qkv_forward(
            scal, xhats, lnv[layer], qkv_b[layer][None, :], cosine, sine, pieces["qkv", layer]
        )
        kv_far = swap(kv, "ctx", 1)
        act, slope = hidden_forward(scal, a2e, a2o, fc1_b[layer][None, :], pieces["fc1", layer])
        ctx, lse = attend(q, kv, kv_far, marks)
        parts = branch_out(scal, ctx, act, pieces["dense", layer], pieces["fc2", layer], groups)
        arrived = [swap(parts[k], "tp", k) for k in range(1, groups)]
        saved.append((xhats, hidden, q, kv, kv_far, a1e, a1o, a2e, a2o, act, slope, ctx, lse))
        if layer + 1 < LAYERS:
            hidden, mine = add_norm(hidden, parts[0], arrived, outv[layer], False)
            xhats = [mine] + [swap(mine, "tp", k) for k in range(1, groups)]
        else:
            (mine,) = add_norm(hidden, parts[0], arrived, outv[layer], True)
            final = place_rows(order, rows, [mine] + [swap(mine, "tp", k) for k in range(1, groups)])

    dys, grad = [dy], dy[:tp_rows]
    grads = {m: None for m in matrices}
    feature_sums, column_sums = [None] * LAYERS, [None] * LAYERS
    for layer in reversed(range(LAYERS)):
        xhats, hidden, q, kv, kv_far, a1e, a1o, a2e, a2o, act, slope, ctx, lse = saved[layer]
        dfc, fc1_sum, grad_ctx, dye, dyo = hidden_back(scal, dys, slope, pieces["fc2", layer], pieces["dense", layer])
        dq, dq_sum, near, away = attend_back(q, kv, kv_far, grad_ctx, lse, marks, cosine, sine)
        dqkv, qkv_sum = join_qkv_grads(dq, dq_sum, near, swap(away, "ctx", 1), cosine, sine)
        *parts, sums = normed_grads(
            scal, dqkv, dfc, xhats, lnv[layer], pieces["qkv", layer], pieces["fc1", layer], groups
        )
        arrived = [swap(parts[k], "tp", k) for k in range(1, groups)]
        back = norm_back(grad, hidden, parts[0], arrived, layer == 0)
        mine = back[1]
        around = [mine] + [swap(mine, "tp", k) for k in range(1, groups)]
        feature_sums[layer] = jnp.concatenate([sums, back[0]], axis=0)
        column_sums[layer] = jnp.concatenate([qkv_sum, fc1_sum], axis=1)

        far = lambda a: swap(a, "fsdp", 1)
        operands = {
            "fc2": (dye, far(dyo), act, far(act)),
            "dense": (dye, None, ctx, far(ctx)),
            "fc1": (a2e, far(a2o), dfc, far(dfc)),
            "qkv": (a1e, far(a1o), dqkv, far(dqkv)),
        }
        operands["dense"] = (dye, operands["fc2"][1], *operands["dense"][2:])
        other_rows = width // 2 - block
        for m, (left, left_far, right, right_far) in operands.items():
            got = []
            if other_rows:
                away_rows = weight_grad(
                    scal, left, left_far, block, other_rows, right, right_far, [],
                    block // 2 if share else other_rows, "grad_away",
                )
                for i, j in enumerate(js[1 : shards // 2]):
                    piece = away_rows if other_rows == block else away_rows[i * block : (i + 1) * block]
                    got.append(swap(piece, "fsdp", j))
            mine_rows = weight_grad(scal, left, left_far, 0, block, right, right_far, got, block, "grad_own")
            grads[m] = finish_grad(mine_rows, swap(mine_rows, "ctx", 1), layer, grads[m])
        if layer > 0:
            dys, grad = around, back[2]
        else:
            input_grad = place_rows(order, rows, around)

    features = reorder(jnp.concatenate(feature_sums, axis=0), back_order)
    columns = jnp.concatenate(column_sums, axis=0)
    lead = features.shape[0]
    both = jnp.concatenate([features.reshape(1, -1), columns.reshape(1, -1)], axis=1)

    def summed(values, axis, size):
        bit = 1
        while bit < size:
            values = values + swap(values, axis, bit)
            bit *= 2
        return values

    both = summed(both, "fsdp", shards)
    both = summed(both, "ctx", sides)
    features = summed(both[:, : lead * width], "tp", groups).reshape(LAYERS, 5, width)
    columns = both[:, lead * width :].reshape(LAYERS, -1)
    qkv_cols = qkv_b.shape[1]
    out_b_grad = jnp.stack([features[:, 4], features[:, 4]], axis=1)
    return (
        final,
        input_grad,
        features[:, 0:2],
        features[:, 2:4],
        grads["qkv"],
        columns[:, :qkv_cols],
        grads["dense"],
        out_b_grad,
        grads["fc1"],
        columns[:, qkv_cols:],
        grads["fc2"],
    )


def solution(mesh):
    by_token = P(("fsdp", "ctx"), None)
    matrix = P(None, "fsdp", "tp")
    vector = P(None, "tp")
    in_specs = (
        by_token, P("fsdp", None), P(), P(), matrix, vector, matrix, P(), matrix, vector, matrix, by_token,
    )
    out_specs = (by_token, by_token, P(), P(), matrix, vector, matrix, P(), matrix, vector, matrix)
    return jax.shard_map(per_device, mesh=mesh, in_specs=in_specs, out_specs=out_specs, check_vma=False)
```
